512 devices in a mesh: ctx: 64 (over x, z, core), kvh: 8 (over y).
Axes of the slice: x: 4, y: 8, z: 8, core: 2. Of those that a mesh axis runs over, the one named last changes fastest.
Arguments:
- queries: bfloat16 [32768, 8192], P('ctx', 'kvh')
- key_vector_rows: bfloat16 [32768, 1024], P('ctx', 'kvh')
- value_vector_rows: bfloat16 [32768, 1024], P('ctx', 'kvh'), may hold values from -6 to 6
- block_picks: int32 [256, 8], P('ctx'), may hold values from 0 to 255, as said below
Outputs:
- attended: bfloat16 [32768, 8192], P(('ctx', 'kvh'))
The draws below stay inside these ranges and needn't reach their ends.
Inputs may be any that keep to these rules, and one draw needn't show every extreme that they name: block_picks[b, 0] = b. The other entries of a row name 7 distinct blocks that lie on other indices of ctx (block c lies on index c // 4). Over the 4 rows of one index of ctx, the entries naming blocks of any one other index are at most 2 and name at most 1 distinct blocks; both bounds are reached in every draw.
All inputs are finite; a program needn't handle non-finite values.
Results may differ from the reference program's by a relative error of at most 0.0047.
Values may be sent and summed in bfloat16 or wider, within the bound.
No kernel may reach another device: no remote copies, remote signals or barrier semaphores. Data moves between devices by JAX's collectives and lax.ppermute only.
A program may use at most 64 MiB of HBM per device.

```python
import math
import jax
import jax.numpy as jnp
from jax import lax

H = 64
KEY_VALUE_HEADS = 8
HEAD_SIZE = 128
BLOCK_TOKENS = 128
PICKED_BLOCKS = 8
SEQUENCE_TOKENS = 32768
BPD = 4
SEQUENCE_BLOCKS = 256
QUERY_PER_GROUP = 8
REMOTE = 28
CAPD = 1
N_CTX = 64


def draw_key_vector_rows(key, part):
    renewed_key = jax.random.fold_in(key, 1)
    field_value = jnp.clip(jax.random.normal(renewed_key, (SEQUENCE_TOKENS, KEY_VALUE_HEADS, HEAD_SIZE), jnp.float32), -6.0, 6.0)
    return field_value.reshape(SEQUENCE_TOKENS, KEY_VALUE_HEADS * HEAD_SIZE).astype(jnp.bfloat16)


def draw_queries(key, part):
    renewed_key = jax.random.fold_in(key, 2)
    field_value = jnp.clip(jax.random.normal(renewed_key, (SEQUENCE_TOKENS, KEY_VALUE_HEADS, QUERY_PER_GROUP, HEAD_SIZE), jnp.float32), -6.0, 6.0)
    return field_value.reshape(SEQUENCE_TOKENS, H * HEAD_SIZE).astype(jnp.bfloat16)


def local_permutation(one_key):
    return jax.random.permutation(one_key, BPD)


def draw_block_picks(key, part):
    total_slots = (N_CTX - 1) * CAPD
    lowest = max(CAPD, REMOTE - total_slots)

    def one_device(device):
        device_key = jax.random.fold_in(key, device + 100)
        keys_five = jax.random.split(device_key, 5)
        others = (device + 1 + jax.random.permutation(keys_five[0], N_CTX - 1)) % N_CTX
        rest = CAPD + jax.random.permutation(keys_five[1], (N_CTX - 2) * CAPD)
        sequence = jnp.concatenate([jnp.arange(CAPD, dtype=jnp.int32), rest.astype(jnp.int32)])
        doubled = jax.random.randint(keys_five[2], (), lowest, REMOTE // 2 + 1)
        distinct_count = REMOTE - doubled
        positions = jnp.arange(REMOTE, dtype=jnp.int32)
        first_pass = sequence[jnp.minimum(positions, total_slots - 1)]
        second_pass = sequence[jnp.clip(positions - distinct_count, 0, total_slots - 1)]
        slot_ids = jnp.where(positions < distinct_count, first_pass, second_pass)
        owner_slot = slot_ids // CAPD
        copy_index = slot_ids % CAPD
        local_perms = jax.vmap(local_permutation)(jax.random.split(keys_five[3], N_CTX - 1))
        local_ids = local_perms[owner_slot, copy_index]
        block_ids = others[owner_slot] * BPD + local_ids
        grouped = block_ids.reshape(BPD, PICKED_BLOCKS - 1)[jax.random.permutation(keys_five[4], BPD)]
        diagonal = device * BPD + jnp.arange(BPD, dtype=jnp.int32)
        return jnp.concatenate([diagonal[:, None], grouped.astype(jnp.int32)], axis=1)
    rows_all = jax.vmap(one_device)(jnp.arange(N_CTX, dtype=jnp.int32))
    return rows_all.reshape(SEQUENCE_BLOCKS, PICKED_BLOCKS).astype(jnp.int32)


def block_levels(own_key, extent, pieces, least, largest):
    gain, own = 1.0, jax.random.fold_in(own_key, 6)
    for dim, shards_of in pieces:
        heights = jnp.exp(jax.random.uniform(jax.random.fold_in(own, dim), (shards_of,), jnp.float32, least / len(pieces), largest / len(pieces)))
        gain = gain * jnp.repeat(heights, extent[dim] // shards_of).reshape([-1 if axis == dim else 1 for axis in range(len(extent))])
    return gain


def normal_values(key, shape, width, bound, cuts=(), kind=jnp.bfloat16):
    result = jax.random.normal(key, shape, jnp.float32) * width
    if len(cuts) > 0:
        result = block_levels(key, shape, cuts, -0.22, 0.18) * result
    return jnp.clip(result, min=-bound, max=bound).astype(kind)


def setup_inputs(seed: int = 0) -> dict:
    key_list = jax.random.split(jax.random.key(seed), 5)
    return {
        "queries": draw_queries(jax.random.fold_in(key_list[4], 71), 0),
        "key_vector_rows": draw_key_vector_rows(jax.random.fold_in(key_list[4], 71), 0),
        "value_vector_rows": normal_values(key_list[2], (SEQUENCE_TOKENS, KEY_VALUE_HEADS * HEAD_SIZE), 1.0, 6.0, ((0, 64), (1, 8))),
        "block_picks": draw_block_picks(jax.random.fold_in(key_list[4], 71), 0),
    }


def reference(queries, key_vector_rows, value_vector_rows, block_picks):
    score_scale = 1.0 / math.sqrt(HEAD_SIZE)
    blocked_queries = queries.reshape(SEQUENCE_BLOCKS, BLOCK_TOKENS, KEY_VALUE_HEADS, QUERY_PER_GROUP, HEAD_SIZE)
    blocked_keys = key_vector_rows.reshape(SEQUENCE_BLOCKS, BLOCK_TOKENS, KEY_VALUE_HEADS, HEAD_SIZE)
    blocked_values = value_vector_rows.reshape(SEQUENCE_BLOCKS, BLOCK_TOKENS, KEY_VALUE_HEADS, HEAD_SIZE)
    positions = jnp.arange(BLOCK_TOKENS, dtype=jnp.int32)
    causal = positions[None, :] <= positions[:, None]
    visible = jnp.concatenate([causal, jnp.ones((BLOCK_TOKENS, (PICKED_BLOCKS - 1) * BLOCK_TOKENS), dtype=bool)], axis=1)

    def attend_one(pair):
        query_block, picked_row = pair
        key_selection = blocked_keys[picked_row].reshape(PICKED_BLOCKS * BLOCK_TOKENS, KEY_VALUE_HEADS, HEAD_SIZE).astype(jnp.float32)
        value_selection = blocked_values[picked_row].reshape(PICKED_BLOCKS * BLOCK_TOKENS, KEY_VALUE_HEADS, HEAD_SIZE).astype(jnp.float32)
        scores = jnp.einsum('qgxd,kgd->gxqk', query_block.astype(jnp.float32), key_selection) * score_scale
        scores = jnp.where(visible, scores, -jnp.inf)
        row_max = lax.optimization_barrier(jnp.max(scores, axis=-1, keepdims=True))
        exponents = jnp.exp(scores - row_max)
        totals = lax.optimization_barrier(jnp.sum(exponents, axis=-1, keepdims=True))
        weights = lax.optimization_barrier(exponents.astype(jnp.bfloat16)).astype(jnp.float32)
        blended = jnp.einsum('gxqk,kgd->qgxd', weights, value_selection)
        blended = blended / jnp.transpose(totals, (2, 0, 1, 3))
        return blended.reshape(BLOCK_TOKENS, H * HEAD_SIZE).astype(jnp.bfloat16)
    outputs = lax.map(attend_one, (blocked_queries, block_picks.astype(jnp.int32)))
    return outputs.reshape(SEQUENCE_TOKENS, H * HEAD_SIZE)
```

```python
import math

import jax
import jax.numpy as jnp
from jax import lax
from jax.experimental import pallas as pl
from jax.experimental.pallas import tpu as pltpu
from jax.sharding import PartitionSpec as P

HEAD_SIZE = 128
BLOCK_TOKENS = 128
PICKED_BLOCKS = 8


def pick_kernel(wanted, k_ref, v_ref, out_ref, sem):
    peers = out_ref.shape[0]

    def copies(d):
        start = pl.multiple_of(wanted[d] * BLOCK_TOKENS, BLOCK_TOKENS)
        rows = pl.ds(start, BLOCK_TOKENS)
        return (
            pltpu.make_async_copy(
                k_ref.at[rows], out_ref.at[d, pl.ds(0, BLOCK_TOKENS)], sem
            ),
            pltpu.make_async_copy(
                v_ref.at[rows], out_ref.at[d, pl.ds(BLOCK_TOKENS, BLOCK_TOKENS)], sem
            ),
        )

    @pl.loop(0, peers)
    def _(d):
        for copy in copies(d):
            copy.start()

    pltpu.make_async_copy(out_ref, out_ref, sem).wait()


def pick_blocks(wanted, keys, values):
    peers = wanted.shape[0]
    return pl.pallas_call(
        pick_kernel,
        out_shape=jax.ShapeDtypeStruct((peers, 2 * BLOCK_TOKENS, HEAD_SIZE), keys.dtype),
        grid_spec=pltpu.PrefetchScalarGridSpec(
            num_scalar_prefetch=1,
            grid=(1,),
            in_specs=[
                pl.BlockSpec(keys.shape, lambda i, w: (0, 0)),
                pl.BlockSpec(values.shape, lambda i, w: (0, 0)),
            ],
            out_specs=pl.BlockSpec(memory_space=pl.ANY),
            scratch_shapes=[pltpu.SemaphoreType.DMA],
        ),
        name="pick_blocks",
    )(wanted, keys, values)


def attend_kernel(slots, q_ref, k_ref, v_ref, *rest):
    far = rest[: PICKED_BLOCKS - 1]
    out_ref, q_buf, k_buf, v_buf = rest[PICKED_BLOCKS - 1 :]
    heads = q_ref.shape[1] // HEAD_SIZE
    for h in range(heads):
        q_buf[pl.ds(h * BLOCK_TOKENS, BLOCK_TOKENS), :] = q_ref[:, pl.ds(h * HEAD_SIZE, HEAD_SIZE)]
    k_buf[pl.ds(0, BLOCK_TOKENS), :] = k_ref[...]
    v_buf[pl.ds(0, BLOCK_TOKENS), :] = v_ref[...]
    for j, block in enumerate(far):
        rows = pl.ds((j + 1) * BLOCK_TOKENS, BLOCK_TOKENS)
        k_buf[rows, :] = block[0, pl.ds(0, BLOCK_TOKENS), :]
        v_buf[rows, :] = block[0, pl.ds(BLOCK_TOKENS, BLOCK_TOKENS), :]
    factor = math.log2(math.e) / math.sqrt(HEAD_SIZE)
    shape = (BLOCK_TOKENS, BLOCK_TOKENS)
    causal = lax.broadcasted_iota(jnp.int32, shape, 1) <= lax.broadcasted_iota(jnp.int32, shape, 0)
    for h in range(heads):
        scores = lax.dot_general(
            q_buf[pl.ds(h * BLOCK_TOKENS, BLOCK_TOKENS), :],
            k_buf[...],
            (((1,), (1,)), ((), ())),
            preferred_element_type=jnp.float32,
        )
        own = jnp.where(causal, scores[:, :BLOCK_TOKENS], -jnp.inf)
        scores = jnp.concatenate([own, scores[:, BLOCK_TOKENS:]], axis=1)
        row_max = jnp.max(scores, axis=1, keepdims=True)
        exponents = jnp.exp2((scores - row_max) * factor)
        totals = jnp.sum(exponents, axis=1, keepdims=True)
        blended = jnp.dot(
            exponents.astype(jnp.bfloat16), v_buf[...], preferred_element_type=jnp.float32
        )
        out_ref[:, pl.ds(h * HEAD_SIZE, HEAD_SIZE)] = (blended / totals).astype(out_ref.dtype)


def attend(slots, queries, keys, values, fetched):
    rows, width = queries.shape
    blocks = rows // BLOCK_TOKENS
    span = PICKED_BLOCKS * BLOCK_TOKENS

    def far_spec(j):
        return pl.BlockSpec(
            (1, 2 * BLOCK_TOKENS, HEAD_SIZE), lambda i, s: (s[i * PICKED_BLOCKS + j], 0, 0)
        )

    return pl.pallas_call(
        attend_kernel,
        out_shape=jax.ShapeDtypeStruct((rows, width), jnp.bfloat16),
        grid_spec=pltpu.PrefetchScalarGridSpec(
            num_scalar_prefetch=1,
            grid=(blocks,),
            in_specs=[
                pl.BlockSpec((BLOCK_TOKENS, width), lambda i, s: (i, 0)),
                pl.BlockSpec((BLOCK_TOKENS, HEAD_SIZE), lambda i, s: (i, 0)),
                pl.BlockSpec((BLOCK_TOKENS, HEAD_SIZE), lambda i, s: (i, 0)),
            ]
            + [far_spec(j) for j in range(1, PICKED_BLOCKS)],
            out_specs=pl.BlockSpec((BLOCK_TOKENS, width), lambda i, s: (i, 0)),
            scratch_shapes=[
                pltpu.VMEM((width // HEAD_SIZE * BLOCK_TOKENS, HEAD_SIZE), jnp.bfloat16),
                pltpu.VMEM((span, HEAD_SIZE), jnp.bfloat16),
                pltpu.VMEM((span, HEAD_SIZE), jnp.bfloat16),
            ],
        ),
        name="attend",
    )(slots, queries, keys, values, *([fetched] * (PICKED_BLOCKS - 1)))


def body(queries, key_vector_rows, value_vector_rows, block_picks):
    peers = lax.axis_size("ctx")
    tok_dev = key_vector_rows.shape[0]
    blocks = tok_dev // BLOCK_TOKENS
    owners = block_picks // blocks
    local_ids = block_picks % blocks
    far_owners = owners[:, 1:].reshape(-1)
    far_ids = local_ids[:, 1:].reshape(-1)
    hits = far_owners[None, :] == jnp.arange(peers, dtype=jnp.int32)[:, None]
    requests = jnp.max(jnp.where(hits, far_ids[None, :], 0), axis=1)
    wanted = lax.all_to_all(requests, "ctx", split_axis=0, concat_axis=0, tiled=True)
    outgoing = pick_blocks(wanted, key_vector_rows, value_vector_rows)
    incoming = lax.all_to_all(outgoing, "ctx", split_axis=0, concat_axis=0, tiled=True)
    attended = attend(
        owners.reshape(-1), queries, key_vector_rows, value_vector_rows, incoming
    )
    return lax.all_to_all(attended, "kvh", split_axis=0, concat_axis=1, tiled=True)


def solution(mesh):
    return jax.shard_map(
        body,
        mesh=mesh,
        in_specs=(P("ctx", "kvh"), P("ctx", "kvh"), P("ctx", "kvh"), P("ctx", None)),
        out_specs=P(("ctx", "kvh"), None),
        check_vma=False,
    )
```

```python
import math

import jax
import jax.numpy as jnp
from jax import lax
from jax.experimental import pallas as pl
from jax.experimental.pallas import tpu as pltpu
from jax.sharding import PartitionSpec as P

HEAD_SIZE = 128
BLOCK_TOKENS = 128
PICKED_BLOCKS = 8
SIZE_X, SIZE_Z, CORES = 4, 8, 2
STEPS = (0, 1, 7, 2, 6, 3, 5, 4)
BATCHES = ((0, 1, 2), (3, 4, 5, 6, 7))


def pick_kernel(slots, wanted, *refs):
    shards, out_ref, sem = refs[:-2], refs[-2], refs[-1]
    half = shards[0].shape[0] // 2

    @pl.loop(0, out_ref.shape[0])
    def _(d):
        for n, (slot, shard) in enumerate(zip(slots, shards)):
            start = wanted[d * SIZE_Z + slot] * BLOCK_TOKENS
            for part in range(2):
                rows = pl.ds(pl.multiple_of(part * half + start, BLOCK_TOKENS), BLOCK_TOKENS)
                target = out_ref.at[d, n, pl.ds(part * BLOCK_TOKENS, BLOCK_TOKENS)]
                pltpu.make_async_copy(shard.at[rows], target, sem).start()

    pltpu.make_async_copy(out_ref, out_ref, sem).wait()


def pick_blocks(wanted, slots, shards):
    group = SIZE_X * CORES
    shape = (group, len(slots), 2 * BLOCK_TOKENS, HEAD_SIZE)
    return pl.pallas_call(
        lambda *refs: pick_kernel(slots, *refs),
        out_shape=jax.ShapeDtypeStruct(shape, shards[0].dtype),
        grid_spec=pltpu.PrefetchScalarGridSpec(
            num_scalar_prefetch=1,
            grid=(1,),
            in_specs=[pl.BlockSpec(s.shape, lambda i, w: (0, 0)) for s in shards],
            out_specs=pl.BlockSpec(memory_space=pl.ANY),
            scratch_shapes=[pltpu.SemaphoreType.DMA],
        ),
        cost_estimate=pl.CostEstimate(flops=0, bytes_accessed=2 * 2 * math.prod(shape), transcendentals=0),
        name="pick_blocks",
    )(wanted, *shards)


def attend_kernel(sizes, places, q_ref, k_ref, v_ref, *rest):
    fetched = rest[: len(sizes)]
    out_ref, q_buf, k_buf, v_buf, k_sem, v_sem = rest[len(sizes) :]
    row = pl.program_id(0)
    heads = q_ref.shape[1] // HEAD_SIZE

    def start(source, r, j):
        rows = pl.ds(j * BLOCK_TOKENS, BLOCK_TOKENS)
        pltpu.make_async_copy(source(0), k_buf.at[r, rows], k_sem.at[r]).start()
        pltpu.make_async_copy(source(1), v_buf.at[r, rows], v_sem.at[r]).start()

    @pl.when(row == 0)
    def _():
        for r in range(k_buf.shape[0]):
            own = pl.ds(r * BLOCK_TOKENS, BLOCK_TOKENS)
            start(lambda part: (k_ref, v_ref)[part].at[own], r, 0)
            for j in range(1, PICKED_BLOCKS):
                place = places[r * PICKED_BLOCKS + j]
                column, slot = place // SIZE_Z, place % SIZE_Z
                first = 0
                for ref, size in zip(fetched, sizes):
                    def go(ref=ref, first=first, r=r, j=j, column=column, slot=slot):
                        start(lambda part: ref.at[column, slot - first, pl.ds(part * BLOCK_TOKENS, BLOCK_TOKENS)], r, j)

                    if len(sizes) == 1:
                        go()
                    else:
                        pl.when((slot >= first) & (slot < first + size))(go)
                    first += size

    for h in range(heads):
        q_buf[pl.ds(h * BLOCK_TOKENS, BLOCK_TOKENS), :] = q_ref[:, pl.ds(h * HEAD_SIZE, HEAD_SIZE)]
    pltpu.make_async_copy(k_buf.at[row], k_buf.at[row], k_sem.at[row]).wait()
    pltpu.make_async_copy(v_buf.at[row], v_buf.at[row], v_sem.at[row]).wait()
    factor = math.log2(math.e) / math.sqrt(HEAD_SIZE)
    PAIR = 2
    shape = (PAIR * BLOCK_TOKENS, BLOCK_TOKENS)
    causal = lax.broadcasted_iota(jnp.int32, shape, 1) <= lax.broadcasted_iota(jnp.int32, shape, 0) % BLOCK_TOKENS
    for h in range(0, heads, PAIR):
        scores = lax.dot_general(
            q_buf[pl.ds(h * BLOCK_TOKENS, PAIR * BLOCK_TOKENS), :],
            k_buf[row],
            (((1,), (1,)), ((), ())),
            preferred_element_type=jnp.float32,
        )
        own = jnp.where(causal, scores[:, :BLOCK_TOKENS], -jnp.inf)
        scores = jnp.concatenate([own, scores[:, BLOCK_TOKENS:]], axis=1)
        row_max = jnp.max(scores, axis=1, keepdims=True)
        exponents = jnp.exp2((scores - row_max) * factor)
        totals = jnp.sum(exponents, axis=1, keepdims=True)
        blended = jnp.dot(exponents.astype(jnp.bfloat16), v_buf[row], preferred_element_type=jnp.float32)
        result = (blended / totals).astype(out_ref.dtype)
        for n in range(PAIR):
            out_ref[:, pl.ds((h + n) * HEAD_SIZE, HEAD_SIZE)] = result[n * BLOCK_TOKENS : (n + 1) * BLOCK_TOKENS]


def attend(places, queries, keys, values, fetched):
    rows, width = queries.shape
    blocks = rows // BLOCK_TOKENS
    span = PICKED_BLOCKS * BLOCK_TOKENS
    sizes = [f.shape[1] for f in fetched]
    anywhere = pl.BlockSpec(memory_space=pl.ANY)
    return pl.pallas_call(
        lambda *refs: attend_kernel(sizes, *refs),
        out_shape=jax.ShapeDtypeStruct((rows, width), jnp.bfloat16),
        grid_spec=pltpu.PrefetchScalarGridSpec(
            num_scalar_prefetch=1,
            grid=(blocks,),
            in_specs=[pl.BlockSpec((BLOCK_TOKENS, width), lambda i, s: (i, 0))] + [anywhere] * (2 + len(fetched)),
            out_specs=pl.BlockSpec((BLOCK_TOKENS, width), lambda i, s: (i, 0)),
            scratch_shapes=[
                pltpu.VMEM((width // HEAD_SIZE * BLOCK_TOKENS, HEAD_SIZE), jnp.bfloat16),
                pltpu.VMEM((blocks, span, HEAD_SIZE), jnp.bfloat16),
                pltpu.VMEM((blocks, span, HEAD_SIZE), jnp.bfloat16),
                pltpu.SemaphoreType.DMA((blocks,)),
                pltpu.SemaphoreType.DMA((blocks,)),
            ],
        ),
        name="attend",
    )(places, queries, keys, values, *fetched)


def flat(x, z, c):
    return (x % SIZE_X * SIZE_Z + z % SIZE_Z) * CORES + c


CHIPS = [(x, z, c) for x in range(SIZE_X) for z in range(SIZE_Z) for c in range(CORES)]
UP = [(flat(x, z, c), flat(x, z + 1, c)) for x, z, c in CHIPS]
DOWN = [(flat(x, z, c), flat(x, z - 1, c)) for x, z, c in CHIPS]
LAST = [(flat(x, z, c), flat(x, z + 1 - 2 * c, c)) for x, z, c in CHIPS]
ROWS = [[flat(x, z, c) for x in range(SIZE_X) for c in range(CORES)] for z in range(SIZE_Z)]


def to_row(array):
    return lax.all_to_all(array, "ctx", split_axis=0, concat_axis=0, axis_index_groups=ROWS, tiled=True)


def body(queries, key_vector_rows, value_vector_rows, block_picks):
    blocks = key_vector_rows.shape[0] // BLOCK_TOKENS
    group = SIZE_X * CORES
    me = lax.axis_index("ctx")
    my_z, my_core = me // CORES % SIZE_Z, me % CORES
    owners, local_ids = block_picks // blocks, block_picks % blocks
    column = owners // (SIZE_Z * CORES) * CORES + owners % CORES
    behind = (my_z - owners // CORES) % SIZE_Z
    slot = jnp.zeros_like(behind)
    for s, step in enumerate(STEPS):
        slot = jnp.where(behind == step, s, slot)
    places = column * SIZE_Z + slot
    far, far_ids = places[:, 1:].reshape(1, -1), local_ids[:, 1:].reshape(1, -1)
    hits = far == jnp.arange(group * SIZE_Z, dtype=jnp.int32)[:, None]
    requests = jnp.max(jnp.where(hits, far_ids, 0), axis=1).reshape(group, SIZE_Z)
    wanted = to_row(requests).reshape(-1)

    shard = jnp.concatenate([key_vector_rows, value_vector_rows], axis=0)
    held = {0: shard}
    for d in range(1, 4):
        held[d] = lax.ppermute(held[d - 1], "ctx", UP)
        held[8 - d] = lax.ppermute(held[(9 - d) % 8], "ctx", DOWN)
    held[4] = lax.ppermute(jnp.where(my_core == 0, held[3], held[5]), "ctx", LAST)

    fetched = []
    for slots in BATCHES:
        outgoing = pick_blocks(wanted, slots, [held[STEPS[s]] for s in slots])
        fetched.append(to_row(outgoing))
    attended = attend(places.reshape(-1), queries, key_vector_rows, value_vector_rows, fetched)
    return lax.all_to_all(attended, "kvh", split_axis=0, concat_axis=1, tiled=True)


def solution(mesh):
    return jax.shard_map(
        body,
        mesh=mesh,
        in_specs=(P("ctx", "kvh"), P("ctx", "kvh"), P("ctx", "kvh"), P("ctx", None)),
        out_specs=P(("ctx", "kvh"), None),
        check_vma=False,
    )
```

```python
import math

import jax
import jax.numpy as jnp
from jax import lax
from jax.experimental import pallas as pl
from jax.experimental.pallas import tpu as pltpu
from jax.sharding import PartitionSpec as P


HEAD_SIZE = 128
BLOCK_TOKENS = 128
PICKED_BLOCKS = 8
SIZE_X, SIZE_Z, CORES = 4, 8, 2
BATCHES = ((0, 1, 2), (3, 4, 5, 6, 7))


def pack_kernel(k_ref, v_ref, out_ref, sem):
    for b in range(out_ref.shape[0]):
        rows = pl.ds(b * BLOCK_TOKENS, BLOCK_TOKENS)
        for part, ref in enumerate((k_ref, v_ref)):
            target = out_ref.at[b, pl.ds(part * BLOCK_TOKENS, BLOCK_TOKENS)]
            pltpu.make_async_copy(ref.at[rows], target, sem).start()
    pltpu.make_async_copy(out_ref, out_ref, sem).wait()


def pack(keys, values):
    rows, width = keys.shape
    return pl.pallas_call(
        pack_kernel,
        out_shape=jax.ShapeDtypeStruct((rows // BLOCK_TOKENS, 2 * BLOCK_TOKENS, width), keys.dtype),
        in_specs=[pl.BlockSpec(memory_space=pl.ANY)] * 2,
        out_specs=pl.BlockSpec(memory_space=pltpu.VMEM),
        scratch_shapes=[pltpu.SemaphoreType.DMA],
        compiler_params=pltpu.CompilerParams(vmem_limit_bytes=PACK_GRANT),
        cost_estimate=pl.CostEstimate(flops=0, bytes_accessed=8 * rows * width, transcendentals=0),
        name="pack",
    )(keys, values)


def pick_kernel(slots, sources, wanted, *refs):
    shards, out_ref = refs[:-1], refs[-1]

    @pl.loop(0, out_ref.shape[0])
    def _(d):
        for n, (slot, (which, first)) in enumerate(zip(slots, sources)):
            out_ref[d, n] = shards[which][first + wanted[d, slot]]


GRANT = 16 * 2**20
PACK_GRANT = 60 * 2**20
ATTEND_GRANT = 48 * 2**20


def pick_blocks(wanted, slots, sources, shards):
    group = SIZE_X * CORES
    shape = (group, len(slots), 2 * BLOCK_TOKENS, HEAD_SIZE)
    return pl.pallas_call(
        lambda *refs: pick_kernel(slots, sources, *refs),
        out_shape=jax.ShapeDtypeStruct(shape, shards[0].dtype),
        grid_spec=pltpu.PrefetchScalarGridSpec(
            num_scalar_prefetch=1,
            in_specs=[pl.BlockSpec(memory_space=pltpu.VMEM)] * len(shards),
            out_specs=pl.BlockSpec(memory_space=pltpu.VMEM),
        ),
        compiler_params=pltpu.CompilerParams(vmem_limit_bytes=GRANT),
        cost_estimate=pl.CostEstimate(flops=0, bytes_accessed=4 * math.prod(shape), transcendentals=0),
        name="pick_blocks",
    )(wanted, *shards)


def attend_kernel(sizes, places, q_ref, k_ref, v_ref, *rest):
    fetched = rest[: len(sizes)]
    out_ref, q_buf, kv_buf, sem = rest[len(sizes) :]
    row = pl.program_id(0)
    heads = q_ref.shape[1] // HEAD_SIZE

    def fetch(r):
        side = lax.rem(r, 2)
        own = pl.ds(pl.multiple_of(r * BLOCK_TOKENS, BLOCK_TOKENS), BLOCK_TOKENS)
        for part, ref in enumerate((k_ref, v_ref)):
            target = kv_buf.at[side, 0, pl.ds(part * BLOCK_TOKENS, BLOCK_TOKENS)]
            pltpu.make_async_copy(ref.at[own], target, sem.at[side]).start()
        for j in range(1, PICKED_BLOCKS):
            place = places[r * PICKED_BLOCKS + j]
            column, slot = place // SIZE_Z, place % SIZE_Z
            first = 0
            for ref, size in zip(fetched, sizes):

                @pl.when((slot >= first) & (slot < first + size))
                def _(ref=ref, first=first):
                    source = ref.at[column, slot - first]
                    pltpu.make_async_copy(source, kv_buf.at[side, j], sem.at[side]).start()

                first += size

    @pl.when(row == 0)
    def _():
        fetch(0)

    for h in range(heads):
        q_buf[pl.ds(h * BLOCK_TOKENS, BLOCK_TOKENS), :] = q_ref[:, pl.ds(h * HEAD_SIZE, HEAD_SIZE)]
    side = lax.rem(row, 2)
    pltpu.make_async_copy(kv_buf.at[side], kv_buf.at[side], sem.at[side]).wait()

    @pl.when(row + 1 < pl.num_programs(0))
    def _():
        fetch(row + 1)

    span = PICKED_BLOCKS * BLOCK_TOKENS
    keys = kv_buf[side, :, pl.ds(0, BLOCK_TOKENS), :].reshape(span, HEAD_SIZE)
    values = kv_buf[side, :, pl.ds(BLOCK_TOKENS, BLOCK_TOKENS), :].reshape(span, HEAD_SIZE)
    factor = math.log2(math.e) / math.sqrt(HEAD_SIZE)
    PAIR = 2
    shape = (PAIR * BLOCK_TOKENS, BLOCK_TOKENS)
    causal = lax.broadcasted_iota(jnp.int32, shape, 1) <= lax.broadcasted_iota(jnp.int32, shape, 0) % BLOCK_TOKENS
    for h in range(0, heads, PAIR):
        scores = lax.dot_general(
            q_buf[pl.ds(h * BLOCK_TOKENS, PAIR * BLOCK_TOKENS), :],
            keys,
            (((1,), (1,)), ((), ())),
            preferred_element_type=jnp.float32,
        )
        own = jnp.where(causal, scores[:, :BLOCK_TOKENS], -jnp.inf)
        scores = jnp.concatenate([own, scores[:, BLOCK_TOKENS:]], axis=1)
        row_max = jnp.max(scores, axis=1, keepdims=True)
        exponents = jnp.exp2((scores - row_max) * factor)
        totals = jnp.sum(exponents, axis=1, keepdims=True)
        blended = jnp.dot(exponents.astype(jnp.bfloat16), values, preferred_element_type=jnp.float32)
        result = (blended / totals).astype(out_ref.dtype)
        for n in range(PAIR):
            out_ref[:, pl.ds((h + n) * HEAD_SIZE, HEAD_SIZE)] = result[n * BLOCK_TOKENS : (n + 1) * BLOCK_TOKENS]


def attend(places, queries, keys, values, fetched):
    rows, width = queries.shape
    blocks = rows // BLOCK_TOKENS
    sizes = [f.shape[1] for f in fetched]
    anywhere = pl.BlockSpec(memory_space=pl.ANY)
    return pl.pallas_call(
        lambda *refs: attend_kernel(sizes, *refs),
        out_shape=jax.ShapeDtypeStruct((rows, width), jnp.bfloat16),
        grid_spec=pltpu.PrefetchScalarGridSpec(
            num_scalar_prefetch=1,
            grid=(blocks,),
            in_specs=[pl.BlockSpec((BLOCK_TOKENS, width), lambda i, s: (i, 0))] + [anywhere] * (2 + len(fetched)),
            out_specs=pl.BlockSpec((BLOCK_TOKENS, width), lambda i, s: (i, 0)),
            scratch_shapes=[
                pltpu.VMEM((width // HEAD_SIZE * BLOCK_TOKENS, HEAD_SIZE), jnp.bfloat16),
                pltpu.VMEM((2, PICKED_BLOCKS, 2 * BLOCK_TOKENS, HEAD_SIZE), jnp.bfloat16),
                pltpu.SemaphoreType.DMA((2,)),
            ],
        ),
        compiler_params=pltpu.CompilerParams(vmem_limit_bytes=ATTEND_GRANT),
        name="attend",
    )(places, queries, keys, values, *fetched)


def flat(x, z, c):
    return (x % SIZE_X * SIZE_Z + z % SIZE_Z) * CORES + c


CHIPS = [(x, z, c) for x in range(SIZE_X) for z in range(SIZE_Z) for c in range(CORES)]
SWAP = [(flat(x, z, c), flat(x, z, 1 - c)) for x, z, c in CHIPS]
STEP = [(flat(x, z, c), flat(x, z + 1 - 2 * c, c)) for x, z, c in CHIPS]
ACROSS = [(flat(x, z, c), flat(x, z + 4 - 8 * c, c)) for x, z, c in CHIPS]
ROWS = [[flat(x, z, c) for x in range(SIZE_X) for c in range(CORES)] for z in range(SIZE_Z)]


def to_row(array):
    return lax.all_to_all(array, "ctx", split_axis=0, concat_axis=0, axis_index_groups=ROWS)


def attention(queries, key_vector_rows, value_vector_rows, block_picks):
    blocks = key_vector_rows.shape[0] // BLOCK_TOKENS
    group = SIZE_X * CORES
    my_z = lax.axis_index("ctx") // CORES % SIZE_Z
    owners, local_ids = block_picks // blocks, block_picks % blocks
    owner_x, owner_z, owner_core = owners // (SIZE_Z * CORES), owners // CORES % SIZE_Z, owners % CORES
    behind = (my_z - owner_z) % SIZE_Z
    ahead = behind > SIZE_Z // 2
    steps = jnp.where(ahead, SIZE_Z - behind, behind)
    direct = (behind == 0) | (behind == SIZE_Z // 2)
    holder_core = jnp.where(direct, owner_core, ahead.astype(jnp.int32))
    slot = jnp.where(behind == 0, 0, 2 * steps - 1 + (owner_core ^ holder_core))
    places = (owner_x * CORES + holder_core) * SIZE_Z + slot
    far, far_ids = places[:, 1:].reshape(1, -1), local_ids[:, 1:].reshape(1, -1)
    hits = far == jnp.arange(group * SIZE_Z, dtype=jnp.int32)[:, None]
    requests = jnp.max(jnp.where(hits, far_ids, 0), axis=1).reshape(group, SIZE_Z)
    wanted = to_row(requests)

    shard = pack(key_vector_rows, value_vector_rows)
    other = lax.ppermute(shard, "ctx", SWAP)
    ring = [jnp.concatenate([shard, other], axis=0)]
    for _ in range(1, 4):
        ring.append(lax.ppermute(ring[-1], "ctx", STEP))
    last = lax.ppermute(shard, "ctx", ACROSS)

    origin = {0: (ring[0], 0), 7: (last, 0)}
    for j in range(1, 4):
        origin[2 * j - 1], origin[2 * j] = (ring[j], 0), (ring[j], blocks)
    fetched = []
    for slots in BATCHES:
        arrays, sources = [], []
        for s in slots:
            array, first = origin[s]
            which = next((i for i, a in enumerate(arrays) if a is array), None)
            if which is None:
                which = len(arrays)
                arrays.append(array)
            sources.append((which, first))
        outgoing = pick_blocks(wanted, slots, sources, arrays)
        fetched.append(to_row(outgoing))
    attended = attend(places.reshape(-1), queries, key_vector_rows, value_vector_rows, fetched)
    return lax.all_to_all(attended, "kvh", split_axis=0, concat_axis=1, tiled=True)


def solution(mesh):
    return jax.shard_map(
        attention,
        mesh=mesh,
        in_specs=(P("ctx", "kvh"), P("ctx", "kvh"), P("ctx", "kvh"), P("ctx", None)),
        out_specs=P(("ctx", "kvh"), None),
        check_vma=False,
    )
```

```python
import math

import jax
import jax.numpy as jnp
from jax import lax
from jax.experimental import pallas as pl
from jax.experimental.pallas import tpu as pltpu
from jax.sharding import PartitionSpec as P


HEAD_SIZE = 128
BLOCK_TOKENS = 128
PICKED_BLOCKS = 8
SIZE_X, SIZE_Z, CORES = 4, 8, 2
OFFSETS = (0, 1, -1, -2, 2, 3, -3, -4)
BATCHES = ((0, 1), (2, 3), (4, 5, 6, 7))


def pack_kernel(k_ref, v_ref, out_ref, sem):
    for b in range(out_ref.shape[0]):
        rows = pl.ds(b * BLOCK_TOKENS, BLOCK_TOKENS)
        for part, ref in enumerate((k_ref, v_ref)):
            target = out_ref.at[b, pl.ds(part * BLOCK_TOKENS, BLOCK_TOKENS)]
            pltpu.make_async_copy(ref.at[rows], target, sem).start()
    pltpu.make_async_copy(out_ref, out_ref, sem).wait()


def pack(keys, values):
    rows, width = keys.shape
    return pl.pallas_call(
        pack_kernel,
        out_shape=jax.ShapeDtypeStruct((rows // BLOCK_TOKENS, 2 * BLOCK_TOKENS, width), keys.dtype),
        in_specs=[pl.BlockSpec(memory_space=pl.ANY)] * 2,
        out_specs=pl.BlockSpec(memory_space=pltpu.VMEM),
        scratch_shapes=[pltpu.SemaphoreType.DMA],
        compiler_params=pltpu.CompilerParams(vmem_limit_bytes=PACK_GRANT),
        cost_estimate=pl.CostEstimate(flops=0, bytes_accessed=8 * rows * width, transcendentals=0),
        name="pack",
    )(keys, values)


def pick_kernel(slots, sources, wanted, *refs):
    shards, out_ref = refs[:-1], refs[-1]

    @pl.loop(0, out_ref.shape[0])
    def _(d):
        for n, (slot, (which, first)) in enumerate(zip(slots, sources)):
            out_ref[d, n] = shards[which][first + wanted[d, slot]]


GRANT = 16 * 2**20
PACK_GRANT = 60 * 2**20
ATTEND_GRANT = 48 * 2**20


def pick_blocks(wanted, slots, sources, shards):
    group = SIZE_X * CORES
    shape = (group, len(slots), 2 * BLOCK_TOKENS, HEAD_SIZE)
    return pl.pallas_call(
        lambda *refs: pick_kernel(slots, sources, *refs),
        out_shape=jax.ShapeDtypeStruct(shape, shards[0].dtype),
        grid_spec=pltpu.PrefetchScalarGridSpec(
            num_scalar_prefetch=1,
            in_specs=[pl.BlockSpec(memory_space=pltpu.VMEM)] * len(shards),
            out_specs=pl.BlockSpec(memory_space=pltpu.VMEM),
        ),
        compiler_params=pltpu.CompilerParams(vmem_limit_bytes=GRANT),
        cost_estimate=pl.CostEstimate(flops=0, bytes_accessed=4 * math.prod(shape), transcendentals=0),
        name="pick_blocks",
    )(wanted, *shards)


def attend_kernel(batches, table, q_ref, k_ref, v_ref, *rest):
    fetched = rest[:batches]
    out_ref, q_buf, kv_buf, sem = rest[batches:]
    row = pl.program_id(0)
    heads = q_ref.shape[1] // HEAD_SIZE

    def fetch(r):
        side = lax.rem(r, 2)
        own = pl.ds(pl.multiple_of(r * BLOCK_TOKENS, BLOCK_TOKENS), BLOCK_TOKENS)
        for part, ref in enumerate((k_ref, v_ref)):
            target = kv_buf.at[side, 0, pl.ds(part * BLOCK_TOKENS, BLOCK_TOKENS)]
            pltpu.make_async_copy(ref.at[own], target, sem.at[side]).start()
        for j in range(1, PICKED_BLOCKS):
            for n, ref in enumerate(fetched):
                index = table[n, r * PICKED_BLOCKS + j]

                @pl.when(index >= 0)
                def _(ref=ref, index=index):
                    pltpu.make_async_copy(ref.at[index], kv_buf.at[side, j], sem.at[side]).start()

    @pl.when(row == 0)
    def _():
        fetch(0)

    for h in range(heads):
        q_buf[pl.ds(h * BLOCK_TOKENS, BLOCK_TOKENS), :] = q_ref[:, pl.ds(h * HEAD_SIZE, HEAD_SIZE)]
    side = lax.rem(row, 2)
    pltpu.make_async_copy(kv_buf.at[side], kv_buf.at[side], sem.at[side]).wait()

    @pl.when(row + 1 < pl.num_programs(0))
    def _():
        fetch(row + 1)

    span = PICKED_BLOCKS * BLOCK_TOKENS
    keys = kv_buf[side, :, pl.ds(0, BLOCK_TOKENS), :].reshape(span, HEAD_SIZE)
    values = kv_buf[side, :, pl.ds(BLOCK_TOKENS, BLOCK_TOKENS), :].reshape(span, HEAD_SIZE)
    factor = math.log2(math.e) / math.sqrt(HEAD_SIZE)
    PAIR = 2
    shape = (PAIR * BLOCK_TOKENS, BLOCK_TOKENS)
    causal = lax.broadcasted_iota(jnp.int32, shape, 1) <= lax.broadcasted_iota(jnp.int32, shape, 0) % BLOCK_TOKENS

    def score(h):
        return lax.dot_general(
            q_buf[pl.ds(h * BLOCK_TOKENS, PAIR * BLOCK_TOKENS), :],
            keys,
            (((1,), (1,)), ((), ())),
            preferred_element_type=jnp.float32,
        )

    following = score(0)
    for h in range(0, heads, PAIR):
        scores = following
        if h + PAIR < heads:
            following = score(h + PAIR)
        own = jnp.where(causal, scores[:, :BLOCK_TOKENS], -jnp.inf)
        scores = jnp.concatenate([own, scores[:, BLOCK_TOKENS:]], axis=1)
        row_max = jnp.max(scores, axis=1, keepdims=True)
        exponents = jnp.exp2((scores - row_max) * factor)
        totals = jnp.sum(exponents, axis=1, keepdims=True)
        blended = jnp.dot(exponents.astype(jnp.bfloat16), values, preferred_element_type=jnp.float32)
        result = (blended / totals).astype(out_ref.dtype)
        for n in range(PAIR):
            out_ref[:, pl.ds((h + n) * HEAD_SIZE, HEAD_SIZE)] = result[n * BLOCK_TOKENS : (n + 1) * BLOCK_TOKENS]


def attend(column, slot, queries, keys, values, fetched):
    rows, width = queries.shape
    blocks = rows // BLOCK_TOKENS
    table, first = [], 0
    for f in fetched:
        size = f.shape[1]
        inside = (slot >= first) & (slot < first + size)
        table.append(jnp.where(inside, column * size + slot - first, -1))
        first += size
    fetched = [f.reshape(-1, *f.shape[2:]) for f in fetched]
    anywhere = pl.BlockSpec(memory_space=pl.ANY)
    return pl.pallas_call(
        lambda *refs: attend_kernel(len(fetched), *refs),
        out_shape=jax.ShapeDtypeStruct((rows, width), jnp.bfloat16),
        grid_spec=pltpu.PrefetchScalarGridSpec(
            num_scalar_prefetch=1,
            grid=(blocks,),
            in_specs=[pl.BlockSpec((BLOCK_TOKENS, width), lambda i, s: (i, 0))] + [anywhere] * (2 + len(fetched)),
            out_specs=pl.BlockSpec((BLOCK_TOKENS, width), lambda i, s: (i, 0)),
            scratch_shapes=[
                pltpu.VMEM((width // HEAD_SIZE * BLOCK_TOKENS, HEAD_SIZE), jnp.bfloat16),
                pltpu.VMEM((2, PICKED_BLOCKS, 2 * BLOCK_TOKENS, HEAD_SIZE), jnp.bfloat16),
                pltpu.SemaphoreType.DMA((2,)),
            ],
        ),
        compiler_params=pltpu.CompilerParams(vmem_limit_bytes=ATTEND_GRANT),
        name="attend",
    )(jnp.stack([t.reshape(-1) for t in table]), queries, keys, values, *fetched)


def flat(x, z, c):
    return (x % SIZE_X * SIZE_Z + z % SIZE_Z) * CORES + c


CHIPS = [(x, z, c) for x in range(SIZE_X) for z in range(SIZE_Z) for c in range(CORES)]
FIRST = [(flat(x, z, c), flat(x, z + 1 - 2 * ((z + c) % 2), c)) for x, z, c in CHIPS]
SECOND = [(flat(x, z, c), flat(x, z - 1 + 2 * ((z + c) % 2), c)) for x, z, c in CHIPS]
ROWS = [[flat(x, z, c) for x in range(SIZE_X) for c in range(CORES)] for z in range(SIZE_Z)]


def to_row(array):
    return lax.all_to_all(array, "ctx", split_axis=0, concat_axis=0, axis_index_groups=ROWS)


def attention(queries, key_vector_rows, value_vector_rows, block_picks):
    blocks = key_vector_rows.shape[0] // BLOCK_TOKENS
    group = SIZE_X * CORES
    my_z = lax.axis_index("ctx") // CORES % SIZE_Z
    owners, local_ids = block_picks // blocks, block_picks % blocks
    owner_x, owner_z, owner_core = owners // (SIZE_Z * CORES), owners // CORES % SIZE_Z, owners % CORES
    distance = owner_z - my_z
    distance = jnp.where((my_z + owner_core) % 2 == 0, distance, -distance) % SIZE_Z
    slot = jnp.zeros_like(distance)
    for s, d in enumerate(OFFSETS):
        slot = jnp.where(distance == d % SIZE_Z, s, slot)
    column = owner_x * CORES + owner_core
    places = column * SIZE_Z + slot
    far, far_ids = places[:, 1:].reshape(1, -1), local_ids[:, 1:].reshape(1, -1)
    hits = far == jnp.arange(group * SIZE_Z, dtype=jnp.int32)[:, None]
    requests = jnp.max(jnp.where(hits, far_ids, 0), axis=1).reshape(group, SIZE_Z)
    wanted = to_row(requests)

    shard = pack(key_vector_rows, value_vector_rows)
    other = lax.ppermute(shard, "ctx", FIRST)
    pairs = [jnp.concatenate([shard, other], axis=0)]
    for n in range(1, 4):
        pairs.append(lax.ppermute(pairs[-1], "ctx", SECOND if n % 2 else FIRST))

    origin = {s: (pairs[s // 2], s % 2 * blocks) for s in range(SIZE_Z)}
    fetched = []
    for slots in BATCHES:
        arrays, sources = [], []
        for s in slots:
            array, first = origin[s]
            which = next((i for i, a in enumerate(arrays) if a is array), None)
            if which is None:
                which = len(arrays)
                arrays.append(array)
            sources.append((which, first))
        outgoing = pick_blocks(wanted, slots, sources, arrays)
        fetched.append(to_row(outgoing))
    attended = attend(column, slot, queries, key_vector_rows, value_vector_rows, fetched)
    return lax.all_to_all(attended, "kvh", split_axis=0, concat_axis=1, tiled=True)


def solution(mesh):
    return jax.shard_map(
        attention,
        mesh=mesh,
        in_specs=(P("ctx", "kvh"), P("ctx", "kvh"), P("ctx", "kvh"), P("ctx", None)),
        out_specs=P(("ctx", "kvh"), None),
        check_vma=False,
    )
```

```python
import math

import jax
import jax.numpy as jnp
from jax import lax
from jax.experimental import pallas as pl
from jax.experimental.pallas import tpu as pltpu
from jax.sharding import PartitionSpec as P


HEAD_SIZE = 128
BLOCK_TOKENS = 128
PICKED_BLOCKS = 8
SIZE_X, SIZE_Z, CORES = 4, 8, 2
OFFSETS = (0, 1, -1, -2, 2, 3, -3, -4)
BATCHES = (((0, 1),), ((2, 3, 4, 5), (6, 7)))


def pack_kernel(k_ref, v_ref, out_ref, sem):
    for b in range(out_ref.shape[0]):
        rows = pl.ds(b * BLOCK_TOKENS, BLOCK_TOKENS)
        for part, ref in enumerate((k_ref, v_ref)):
            target = out_ref.at[b, pl.ds(part * BLOCK_TOKENS, BLOCK_TOKENS)]
            pltpu.make_async_copy(ref.at[rows], target, sem).start()
    pltpu.make_async_copy(out_ref, out_ref, sem).wait()


def pack(keys, values):
    rows, width = keys.shape
    return pl.pallas_call(
        pack_kernel,
        out_shape=jax.ShapeDtypeStruct((rows // BLOCK_TOKENS, 2 * BLOCK_TOKENS, width), keys.dtype),
        in_specs=[pl.BlockSpec(memory_space=pl.ANY)] * 2,
        out_specs=pl.BlockSpec(memory_space=pltpu.VMEM),
        scratch_shapes=[pltpu.SemaphoreType.DMA],
        compiler_params=pltpu.CompilerParams(vmem_limit_bytes=PACK_GRANT),
        cost_estimate=pl.CostEstimate(flops=0, bytes_accessed=8 * rows * width, transcendentals=0),
        name="pack",
    )(keys, values)


def pick_kernel(slots, sources, first, wanted, *refs):
    shards, (out_ref, buf, sem) = refs[: max(w for w, _ in sources) + 1], refs[-3:]

    def send(d):
        target = out_ref.at[d, pl.ds(first, len(slots))]
        return pltpu.make_async_copy(buf.at[d], target, sem.at[d])

    @pl.loop(0, buf.shape[0])
    def _(d):
        for n, (slot, (which, begin)) in enumerate(zip(slots, sources)):
            buf[d, n] = shards[which][begin + wanted[d, slot]]
        send(d).start()

    @pl.loop(0, buf.shape[0])
    def _(d):
        send(d).wait()


GRANT = 16 * 2**20
PACK_GRANT = 60 * 2**20
ATTEND_GRANT = 48 * 2**20


def pick_blocks(wanted, slots, sources, shards, first, total, partial):
    group = SIZE_X * CORES
    block = (2 * BLOCK_TOKENS, HEAD_SIZE)
    extra = [] if partial is None else [partial]
    return pl.pallas_call(
        lambda *refs: pick_kernel(slots, sources, first, *refs),
        out_shape=jax.ShapeDtypeStruct((group, total) + block, shards[0].dtype),
        grid_spec=pltpu.PrefetchScalarGridSpec(
            num_scalar_prefetch=1,
            in_specs=[pl.BlockSpec(memory_space=pltpu.VMEM)] * len(shards)
            + [pl.BlockSpec(memory_space=pl.ANY)] * len(extra),
            out_specs=pl.BlockSpec(memory_space=pl.ANY),
            scratch_shapes=[
                pltpu.VMEM((group, len(slots)) + block, shards[0].dtype),
                pltpu.SemaphoreType.DMA((group,)),
            ],
        ),
        input_output_aliases={1 + len(shards): 0} if extra else {},
        compiler_params=pltpu.CompilerParams(vmem_limit_bytes=GRANT),
        cost_estimate=pl.CostEstimate(
            flops=0, bytes_accessed=4 * group * len(slots) * math.prod(block), transcendentals=0
        ),
        name="pick_blocks",
    )(wanted, *shards, *extra)


def attend_kernel(batches, table, q_ref, k_ref, v_ref, *rest):
    fetched = rest[:batches]
    out_ref, q_buf, kv_buf, sem = rest[batches:]
    row = pl.program_id(0)
    heads = q_ref.shape[1] // HEAD_SIZE

    def fetch(r):
        side = lax.rem(r, 2)
        own = pl.ds(pl.multiple_of(r * BLOCK_TOKENS, BLOCK_TOKENS), BLOCK_TOKENS)
        for part, ref in enumerate((k_ref, v_ref)):
            target = kv_buf.at[side, 0, pl.ds(part * BLOCK_TOKENS, BLOCK_TOKENS)]
            pltpu.make_async_copy(ref.at[own], target, sem.at[side]).start()
        for j in range(1, PICKED_BLOCKS):
            for n, ref in enumerate(fetched):
                index = table[n, r * PICKED_BLOCKS + j]

                @pl.when(index >= 0)
                def _(ref=ref, index=index):
                    pltpu.make_async_copy(ref.at[index], kv_buf.at[side, j], sem.at[side]).start()

    @pl.when(row == 0)
    def _():
        fetch(0)

    for h in range(heads):
        q_buf[pl.ds(h * BLOCK_TOKENS, BLOCK_TOKENS), :] = q_ref[:, pl.ds(h * HEAD_SIZE, HEAD_SIZE)]
    side = lax.rem(row, 2)
    pltpu.make_async_copy(kv_buf.at[side], kv_buf.at[side], sem.at[side]).wait()

    @pl.when(row + 1 < pl.num_programs(0))
    def _():
        fetch(row + 1)

    span = PICKED_BLOCKS * BLOCK_TOKENS
    keys = kv_buf[side, :, pl.ds(0, BLOCK_TOKENS), :].reshape(span, HEAD_SIZE)
    values = kv_buf[side, :, pl.ds(BLOCK_TOKENS, BLOCK_TOKENS), :].reshape(span, HEAD_SIZE)
    factor = math.log2(math.e) / math.sqrt(HEAD_SIZE)
    PAIR = 2
    shape = (PAIR * BLOCK_TOKENS, BLOCK_TOKENS)
    causal = lax.broadcasted_iota(jnp.int32, shape, 1) <= lax.broadcasted_iota(jnp.int32, shape, 0) % BLOCK_TOKENS

    def score(h):
        return lax.dot_general(
            q_buf[pl.ds(h * BLOCK_TOKENS, PAIR * BLOCK_TOKENS), :],
            keys,
            (((1,), (1,)), ((), ())),
            preferred_element_type=jnp.float32,
        )

    following = score(0)
    for h in range(0, heads, PAIR):
        scores = following
        if h + PAIR < heads:
            following = score(h + PAIR)
        own = jnp.where(causal, scores[:, :BLOCK_TOKENS], -jnp.inf)
        scores = jnp.concatenate([own, scores[:, BLOCK_TOKENS:]], axis=1)
        row_max = jnp.max(scores, axis=1, keepdims=True)
        exponents = jnp.exp2((scores - row_max) * factor)
        totals = jnp.sum(exponents, axis=1, keepdims=True)
        blended = jnp.dot(exponents.astype(jnp.bfloat16), values, preferred_element_type=jnp.float32)
        result = (blended / totals).astype(out_ref.dtype)
        for n in range(PAIR):
            out_ref[:, pl.ds((h + n) * HEAD_SIZE, HEAD_SIZE)] = result[n * BLOCK_TOKENS : (n + 1) * BLOCK_TOKENS]


def attend(column, slot, queries, keys, values, fetched):
    rows, width = queries.shape
    blocks = rows // BLOCK_TOKENS
    table, first = [], 0
    for f in fetched:
        size = f.shape[1]
        inside = (slot >= first) & (slot < first + size)
        table.append(jnp.where(inside, column * size + slot - first, -1))
        first += size
    fetched = [f.reshape(-1, *f.shape[2:]) for f in fetched]
    anywhere = pl.BlockSpec(memory_space=pl.ANY)
    return pl.pallas_call(
        lambda *refs: attend_kernel(len(fetched), *refs),
        out_shape=jax.ShapeDtypeStruct((rows, width), jnp.bfloat16),
        grid_spec=pltpu.PrefetchScalarGridSpec(
            num_scalar_prefetch=1,
            grid=(blocks,),
            in_specs=[pl.BlockSpec((BLOCK_TOKENS, width), lambda i, s: (i, 0))] + [anywhere] * (2 + len(fetched)),
            out_specs=pl.BlockSpec((BLOCK_TOKENS, width), lambda i, s: (i, 0)),
            scratch_shapes=[
                pltpu.VMEM((width // HEAD_SIZE * BLOCK_TOKENS, HEAD_SIZE), jnp.bfloat16),
                pltpu.VMEM((2, PICKED_BLOCKS, 2 * BLOCK_TOKENS, HEAD_SIZE), jnp.bfloat16),
                pltpu.SemaphoreType.DMA((2,)),
            ],
        ),
        compiler_params=pltpu.CompilerParams(vmem_limit_bytes=ATTEND_GRANT),
        name="attend",
    )(jnp.stack([t.reshape(-1) for t in table]), queries, keys, values, *fetched)


def flat(x, z, c):
    return (x % SIZE_X * SIZE_Z + z % SIZE_Z) * CORES + c


CHIPS = [(x, z, c) for x in range(SIZE_X) for z in range(SIZE_Z) for c in range(CORES)]
FIRST = [(flat(x, z, c), flat(x, z + 1 - 2 * ((z + c) % 2), c)) for x, z, c in CHIPS]
SECOND = [(flat(x, z, c), flat(x, z - 1 + 2 * ((z + c) % 2), c)) for x, z, c in CHIPS]
ROWS = [[flat(x, z, c) for x in range(SIZE_X) for c in range(CORES)] for z in range(SIZE_Z)]


def to_row(array):
    return lax.all_to_all(array, "ctx", split_axis=0, concat_axis=0, axis_index_groups=ROWS)


def attention(queries, key_vector_rows, value_vector_rows, block_picks):
    blocks = key_vector_rows.shape[0] // BLOCK_TOKENS
    group = SIZE_X * CORES
    my_z = lax.axis_index("ctx") // CORES % SIZE_Z
    owners, local_ids = block_picks // blocks, block_picks % blocks
    owner_x, owner_z, owner_core = owners // (SIZE_Z * CORES), owners // CORES % SIZE_Z, owners % CORES
    distance = owner_z - my_z
    distance = jnp.where((my_z + owner_core) % 2 == 0, distance, -distance) % SIZE_Z
    slot = jnp.zeros_like(distance)
    for s, d in enumerate(OFFSETS):
        slot = jnp.where(distance == d % SIZE_Z, s, slot)
    column = owner_x * CORES + owner_core
    places = column * SIZE_Z + slot
    far, far_ids = places[:, 1:].reshape(1, -1), local_ids[:, 1:].reshape(1, -1)
    hits = far == jnp.arange(group * SIZE_Z, dtype=jnp.int32)[:, None]
    requests = jnp.max(jnp.where(hits, far_ids, 0), axis=1).reshape(group, SIZE_Z)
    wanted = to_row(requests)

    shard = pack(key_vector_rows, value_vector_rows)
    other = lax.ppermute(shard, "ctx", FIRST)
    pairs = [jnp.concatenate([shard, other], axis=0)]
    for n in range(1, 4):
        pairs.append(lax.ppermute(pairs[-1], "ctx", SECOND if n % 2 else FIRST))

    fetched = []
    for parts in BATCHES:
        outgoing, first = None, 0
        for slots in parts:
            used = sorted({s // 2 for s in slots})
            sources = [(used.index(s // 2), s % 2 * blocks) for s in slots]
            outgoing = pick_blocks(
                wanted, slots, sources, [pairs[u] for u in used], first, sum(map(len, parts)), outgoing
            )
            first += len(slots)
        fetched.append(to_row(outgoing))
    attended = attend(column, slot, queries, key_vector_rows, value_vector_rows, fetched)
    return lax.all_to_all(attended, "kvh", split_axis=0, concat_axis=1, tiled=True)


def solution(mesh):
    return jax.shard_map(
        attention,
        mesh=mesh,
        in_specs=(P("ctx", "kvh"), P("ctx", "kvh"), P("ctx", "kvh"), P("ctx", None)),
        out_specs=P(("ctx", "kvh"), None),
        check_vma=False,
    )
```

```python
import functools
import math

import jax
import jax.numpy as jnp
from jax import lax
from jax.experimental import pallas as pl
from jax.experimental.pallas import tpu as pltpu
from jax.sharding import PartitionSpec as P


HEAD_SIZE = 128
BLOCK_TOKENS = 128
PICKED_BLOCKS = 8
SIZE_X, SIZE_Z, CORES = 4, 8, 2
OFFSETS = (0, 1, -1, -2, 2, 3, -3, -4)
BATCHES = ((0, 1), (2, 3), (4, 5, 6, 7))


def pack_kernel(k_ref, v_ref, out_ref, sem):
    for b in range(out_ref.shape[0]):
        rows = pl.ds(b * BLOCK_TOKENS, BLOCK_TOKENS)
        for part, ref in enumerate((k_ref, v_ref)):
            target = out_ref.at[b, pl.ds(part * BLOCK_TOKENS, BLOCK_TOKENS)]
            pltpu.make_async_copy(ref.at[rows], target, sem).start()
    pltpu.make_async_copy(out_ref, out_ref, sem).wait()


def pack(keys, values):
    rows, width = keys.shape
    return pl.pallas_call(
        pack_kernel,
        out_shape=jax.ShapeDtypeStruct((rows // BLOCK_TOKENS, 2 * BLOCK_TOKENS, width), keys.dtype),
        in_specs=[pl.BlockSpec(memory_space=pl.ANY)] * 2,
        out_specs=pl.BlockSpec(memory_space=pltpu.VMEM),
        scratch_shapes=[pltpu.SemaphoreType.DMA],
        compiler_params=pltpu.CompilerParams(vmem_limit_bytes=PACK_GRANT),
        cost_estimate=pl.CostEstimate(flops=0, bytes_accessed=8 * rows * width, transcendentals=0),
        name="pack",
    )(keys, values)


def pick_kernel(slots, sources, wanted, *refs):
    shards, out_ref = refs[:-1], refs[-1]

    @pl.loop(0, out_ref.shape[0])
    def _(d):
        for n, (slot, (which, first)) in enumerate(zip(slots, sources)):
            out_ref[d, n] = shards[which][first + wanted[d, slot]]


GRANT = 16 * 2**20
PACK_GRANT = 60 * 2**20
ATTEND_GRANT = 48 * 2**20


def pick_blocks(wanted, slots, sources, shards):
    group = SIZE_X * CORES
    shape = (group, len(slots), 2 * BLOCK_TOKENS, HEAD_SIZE)
    return pl.pallas_call(
        lambda *refs: pick_kernel(slots, sources, *refs),
        out_shape=jax.ShapeDtypeStruct(shape, shards[0].dtype),
        grid_spec=pltpu.PrefetchScalarGridSpec(
            num_scalar_prefetch=1,
            in_specs=[pl.BlockSpec(memory_space=pltpu.VMEM)] * len(shards),
            out_specs=pl.BlockSpec(memory_space=pltpu.VMEM),
        ),
        compiler_params=pltpu.CompilerParams(vmem_limit_bytes=GRANT),
        cost_estimate=pl.CostEstimate(flops=0, bytes_accessed=4 * math.prod(shape), transcendentals=0),
        name="pick_blocks",
    )(wanted, *shards)


def attend_kernel(batches, table, q_ref, k_ref, v_ref, *rest):
    fetched = rest[:batches]
    out_ref, q_buf, kv_buf, sem = rest[batches:]
    row = pl.program_id(0)
    heads = q_ref.shape[1] // HEAD_SIZE

    def fetch(r):
        side = lax.rem(r, 2)
        own = pl.ds(pl.multiple_of(r * BLOCK_TOKENS, BLOCK_TOKENS), BLOCK_TOKENS)
        for part, ref in enumerate((k_ref, v_ref)):
            target = kv_buf.at[side, 0, pl.ds(part * BLOCK_TOKENS, BLOCK_TOKENS)]
            pltpu.make_async_copy(ref.at[own], target, sem.at[side, 0]).start()
        for j in range(1, PICKED_BLOCKS):
            index = table[batches - 1, r * PICKED_BLOCKS + j]

            @pl.when(index >= 0)
            def _(index=index):
                pltpu.make_async_copy(fetched[-1].at[index], kv_buf.at[side, j], sem.at[side, j]).start()

    @pl.when(row == 0)
    def _():
        fetch(0)

    for h in range(heads):
        q_buf[pl.ds(h * BLOCK_TOKENS, BLOCK_TOKENS), :] = q_ref[:, pl.ds(h * HEAD_SIZE, HEAD_SIZE)]
    side = lax.rem(row, 2)

    @pl.when(row + 1 < pl.num_programs(0))
    def _():
        fetch(row + 1)

    for j in range(1, PICKED_BLOCKS):
        for n, ref in enumerate(fetched[:-1]):
            index = table[n, row * PICKED_BLOCKS + j]

            @pl.when(index >= 0)
            def _(ref=ref, index=index):
                kv_buf[side, j] = ref[index]

    def arrived(j):
        pltpu.make_async_copy(kv_buf.at[side, j], kv_buf.at[side, j], sem.at[side, j]).wait()

    arrived(0)
    for j in range(1, PICKED_BLOCKS):
        pl.when(table[batches - 1, row * PICKED_BLOCKS + j] >= 0)(functools.partial(arrived, j))

    span = PICKED_BLOCKS * BLOCK_TOKENS
    keys = kv_buf[side, :, pl.ds(0, BLOCK_TOKENS), :].reshape(span, HEAD_SIZE)
    values = kv_buf[side, :, pl.ds(BLOCK_TOKENS, BLOCK_TOKENS), :].reshape(span, HEAD_SIZE)
    factor = math.log2(math.e) / math.sqrt(HEAD_SIZE)
    PAIR = 2
    shape = (PAIR * BLOCK_TOKENS, BLOCK_TOKENS)
    causal = lax.broadcasted_iota(jnp.int32, shape, 1) <= lax.broadcasted_iota(jnp.int32, shape, 0) % BLOCK_TOKENS

    def score(h):
        return lax.dot_general(
            q_buf[pl.ds(h * BLOCK_TOKENS, PAIR * BLOCK_TOKENS), :],
            keys,
            (((1,), (1,)), ((), ())),
            preferred_element_type=jnp.float32,
        )

    following = score(0)
    for h in range(0, heads, PAIR):
        scores = following
        if h + PAIR < heads:
            following = score(h + PAIR)
        own = jnp.where(causal, scores[:, :BLOCK_TOKENS], -jnp.inf)
        scores = jnp.concatenate([own, scores[:, BLOCK_TOKENS:]], axis=1)
        row_max = jnp.max(scores, axis=1, keepdims=True)
        exponents = jnp.exp2((scores - row_max) * factor)
        totals = jnp.sum(exponents, axis=1, keepdims=True)
        blended = jnp.dot(exponents.astype(jnp.bfloat16), values, preferred_element_type=jnp.float32)
        result = (blended / totals).astype(out_ref.dtype)
        for n in range(PAIR):
            out_ref[:, pl.ds((h + n) * HEAD_SIZE, HEAD_SIZE)] = result[n * BLOCK_TOKENS : (n + 1) * BLOCK_TOKENS]


def attend(column, slot, queries, keys, values, fetched):
    rows, width = queries.shape
    blocks = rows // BLOCK_TOKENS
    table, first = [], 0
    for f in fetched:
        size = f.shape[1]
        inside = (slot >= first) & (slot < first + size)
        table.append(jnp.where(inside, column * size + slot - first, -1))
        first += size
    fetched = [f.reshape(-1, *f.shape[2:]) for f in fetched]
    anywhere = pl.BlockSpec(memory_space=pl.ANY)
    on_chip = pl.BlockSpec(memory_space=pltpu.VMEM)
    return pl.pallas_call(
        lambda *refs: attend_kernel(len(fetched), *refs),
        out_shape=jax.ShapeDtypeStruct((rows, width), jnp.bfloat16),
        grid_spec=pltpu.PrefetchScalarGridSpec(
            num_scalar_prefetch=1,
            grid=(blocks,),
            in_specs=[pl.BlockSpec((BLOCK_TOKENS, width), lambda i, s: (i, 0))]
            + [anywhere] * 2
            + [on_chip] * (len(fetched) - 1)
            + [anywhere],
            out_specs=pl.BlockSpec((BLOCK_TOKENS, width), lambda i, s: (i, 0)),
            scratch_shapes=[
                pltpu.VMEM((width // HEAD_SIZE * BLOCK_TOKENS, HEAD_SIZE), jnp.bfloat16),
                pltpu.VMEM((2, PICKED_BLOCKS, 2 * BLOCK_TOKENS, HEAD_SIZE), jnp.bfloat16),
                pltpu.SemaphoreType.DMA((2, PICKED_BLOCKS)),
            ],
        ),
        compiler_params=pltpu.CompilerParams(vmem_limit_bytes=ATTEND_GRANT),
        name="attend",
    )(jnp.stack([t.reshape(-1) for t in table]), queries, keys, values, *fetched)


def flat(x, z, c):
    return (x % SIZE_X * SIZE_Z + z % SIZE_Z) * CORES + c


CHIPS = [(x, z, c) for x in range(SIZE_X) for z in range(SIZE_Z) for c in range(CORES)]
FIRST = [(flat(x, z, c), flat(x, z + 1 - 2 * ((z + c) % 2), c)) for x, z, c in CHIPS]
SECOND = [(flat(x, z, c), flat(x, z - 1 + 2 * ((z + c) % 2), c)) for x, z, c in CHIPS]
ROWS = [[flat(x, z, c) for x in range(SIZE_X) for c in range(CORES)] for z in range(SIZE_Z)]


def to_row(array):
    return lax.all_to_all(array, "ctx", split_axis=0, concat_axis=0, axis_index_groups=ROWS)


def attention(queries, key_vector_rows, value_vector_rows, block_picks):
    blocks = key_vector_rows.shape[0] // BLOCK_TOKENS
    group = SIZE_X * CORES
    my_z = lax.axis_index("ctx") // CORES % SIZE_Z
    owners, local_ids = block_picks // blocks, block_picks % blocks
    owner_x, owner_z, owner_core = owners // (SIZE_Z * CORES), owners // CORES % SIZE_Z, owners % CORES
    distance = owner_z - my_z
    distance = jnp.where((my_z + owner_core) % 2 == 0, distance, -distance) % SIZE_Z
    slot = jnp.zeros_like(distance)
    for s, d in enumerate(OFFSETS):
        slot = jnp.where(distance == d % SIZE_Z, s, slot)
    column = owner_x * CORES + owner_core
    places = column * SIZE_Z + slot
    far = places[:, 1:].reshape(-1)
    far_ids = local_ids[:, 1:].reshape(-1)
    index = jnp.arange(group, dtype=jnp.int32)[:, None] * SIZE_Z + jnp.arange(SIZE_Z, dtype=jnp.int32)[None, :]
    requests = jnp.max(jnp.where(far == index[:, :, None], far_ids, 0), axis=2)
    wanted = to_row(requests)

    shard = pack(key_vector_rows, value_vector_rows)
    other = lax.ppermute(shard, "ctx", FIRST)
    pairs = [jnp.concatenate([shard, other], axis=0)]
    for n in range(1, 4):
        pairs.append(lax.ppermute(pairs[-1], "ctx", SECOND if n % 2 else FIRST))

    origin = {s: (pairs[s // 2], s % 2 * blocks) for s in range(SIZE_Z)}
    fetched = []
    for slots in BATCHES:
        arrays, sources = [], []
        for s in slots:
            array, first = origin[s]
            which = next((i for i, a in enumerate(arrays) if a is array), None)
            if which is None:
                which = len(arrays)
                arrays.append(array)
            sources.append((which, first))
        outgoing = pick_blocks(wanted, slots, sources, arrays)
        fetched.append(to_row(outgoing))
    attended = attend(column, slot, queries, key_vector_rows, value_vector_rows, fetched)
    return lax.all_to_all(attended, "kvh", split_axis=0, concat_axis=1, tiled=True)


def solution(mesh):
    return jax.shard_map(
        attention,
        mesh=mesh,
        in_specs=(P("ctx", "kvh"), P("ctx", "kvh"), P("ctx", "kvh"), P("ctx", None)),
        out_specs=P(("ctx", "kvh"), None),
        check_vma=False,
    )
```

```python
import functools
import math

import jax
import jax.numpy as jnp
from jax import lax
from jax.experimental import pallas as pl
from jax.experimental.pallas import tpu as pltpu
from jax.sharding import PartitionSpec as P


HEAD_SIZE = 128
BLOCK_TOKENS = 128
PICKED_BLOCKS = 8
SIZE_X, SIZE_Z, CORES = 4, 8, 2
OFFSETS = (0, 1, -1, -2, 2, 3, -3, -4)
BATCHES = ((0, 1), (2, 3, 4, 5), (6, 7))


def pack_kernel(k_ref, v_ref, out_ref, sem):
    for b in range(out_ref.shape[0]):
        rows = pl.ds(b * BLOCK_TOKENS, BLOCK_TOKENS)
        for part, ref in enumerate((k_ref, v_ref)):
            target = out_ref.at[b, pl.ds(part * BLOCK_TOKENS, BLOCK_TOKENS)]
            pltpu.make_async_copy(ref.at[rows], target, sem).start()
    pltpu.make_async_copy(out_ref, out_ref, sem).wait()


def pack(keys, values):
    rows, width = keys.shape
    return pl.pallas_call(
        pack_kernel,
        out_shape=jax.ShapeDtypeStruct((rows // BLOCK_TOKENS, 2 * BLOCK_TOKENS, width), keys.dtype),
        in_specs=[pl.BlockSpec(memory_space=pl.ANY)] * 2,
        out_specs=pl.BlockSpec(memory_space=pltpu.VMEM),
        scratch_shapes=[pltpu.SemaphoreType.DMA],
        compiler_params=pltpu.CompilerParams(vmem_limit_bytes=PACK_GRANT),
        cost_estimate=pl.CostEstimate(flops=0, bytes_accessed=8 * rows * width, transcendentals=0),
        name="pack",
    )(keys, values)


def pick_kernel(slots, sources, wanted, *refs):
    shards, out_ref = refs[:-1], refs[-1]

    @pl.loop(0, out_ref.shape[0])
    def _(d):
        for n, (slot, (which, first)) in enumerate(zip(slots, sources)):
            out_ref[d, n] = shards[which][first + wanted[d, slot]]


GRANT = 16 * 2**20
PACK_GRANT = 60 * 2**20
ATTEND_GRANT = 48 * 2**20


def pick_blocks(wanted, slots, sources, shards):
    group = SIZE_X * CORES
    shape = (group, len(slots), 2 * BLOCK_TOKENS, HEAD_SIZE)
    return pl.pallas_call(
        lambda *refs: pick_kernel(slots, sources, *refs),
        out_shape=jax.ShapeDtypeStruct(shape, shards[0].dtype),
        grid_spec=pltpu.PrefetchScalarGridSpec(
            num_scalar_prefetch=1,
            in_specs=[pl.BlockSpec(memory_space=pltpu.VMEM)] * len(shards),
            out_specs=pl.BlockSpec(memory_space=pltpu.VMEM),
        ),
        compiler_params=pltpu.CompilerParams(vmem_limit_bytes=GRANT),
        cost_estimate=pl.CostEstimate(flops=0, bytes_accessed=4 * math.prod(shape), transcendentals=0),
        name="pick_blocks",
    )(wanted, *shards)


def attend_kernel(batches, table, q_ref, k_ref, v_ref, *rest):
    fetched = rest[:batches]
    out_ref, q_buf, kv_buf, sem = rest[batches:]
    row = pl.program_id(0)
    heads = q_ref.shape[1] // HEAD_SIZE

    def fetch(r):
        side = lax.rem(r, 2)
        own = pl.ds(pl.multiple_of(r * BLOCK_TOKENS, BLOCK_TOKENS), BLOCK_TOKENS)
        for part, ref in enumerate((k_ref, v_ref)):
            target = kv_buf.at[side, 0, pl.ds(part * BLOCK_TOKENS, BLOCK_TOKENS)]
            pltpu.make_async_copy(ref.at[own], target, sem.at[side, 0]).start()
        for j in range(1, PICKED_BLOCKS):
            index = table[batches - 1, r * PICKED_BLOCKS + j]

            @pl.when(index >= 0)
            def _(index=index):
                pltpu.make_async_copy(fetched[-1].at[index], kv_buf.at[side, j], sem.at[side, j]).start()

    @pl.when(row == 0)
    def _():
        fetch(0)

    for h in range(heads):
        q_buf[pl.ds(h * BLOCK_TOKENS, BLOCK_TOKENS), :] = q_ref[:, pl.ds(h * HEAD_SIZE, HEAD_SIZE)]
    side = lax.rem(row, 2)

    @pl.when(row + 1 < pl.num_programs(0))
    def _():
        fetch(row + 1)

    for j in range(1, PICKED_BLOCKS):
        for n, ref in enumerate(fetched[:-1]):
            index = table[n, row * PICKED_BLOCKS + j]

            @pl.when(index >= 0)
            def _(ref=ref, index=index):
                kv_buf[side, j] = ref[index]

    def arrived(j):
        pltpu.make_async_copy(kv_buf.at[side, j], kv_buf.at[side, j], sem.at[side, j]).wait()

    arrived(0)
    for j in range(1, PICKED_BLOCKS):
        pl.when(table[batches - 1, row * PICKED_BLOCKS + j] >= 0)(functools.partial(arrived, j))

    span = PICKED_BLOCKS * BLOCK_TOKENS
    keys = kv_buf[side, :, pl.ds(0, BLOCK_TOKENS), :].reshape(span, HEAD_SIZE)
    values = kv_buf[side, :, pl.ds(BLOCK_TOKENS, BLOCK_TOKENS), :].reshape(span, HEAD_SIZE)
    factor = math.log2(math.e) / math.sqrt(HEAD_SIZE)
    PAIR = 2
    shape = (PAIR * BLOCK_TOKENS, BLOCK_TOKENS)
    causal = lax.broadcasted_iota(jnp.int32, shape, 1) <= lax.broadcasted_iota(jnp.int32, shape, 0) % BLOCK_TOKENS

    def score(h):
        return lax.dot_general(
            q_buf[pl.ds(h * BLOCK_TOKENS, PAIR * BLOCK_TOKENS), :],
            keys,
            (((1,), (1,)), ((), ())),
            preferred_element_type=jnp.float32,
        )

    following = score(0)
    for h in range(0, heads, PAIR):
        scores = following
        if h + PAIR < heads:
            following = score(h + PAIR)
        own = jnp.where(causal, scores[:, :BLOCK_TOKENS], -jnp.inf)
        scores = jnp.concatenate([own, scores[:, BLOCK_TOKENS:]], axis=1)
        row_max = jnp.max(scores, axis=1, keepdims=True)
        exponents = jnp.exp2((scores - row_max) * factor)
        totals = jnp.sum(exponents, axis=1, keepdims=True)
        blended = jnp.dot(exponents.astype(jnp.bfloat16), values, preferred_element_type=jnp.float32)
        result = (blended / totals).astype(out_ref.dtype)
        for n in range(PAIR):
            out_ref[:, pl.ds((h + n) * HEAD_SIZE, HEAD_SIZE)] = result[n * BLOCK_TOKENS : (n + 1) * BLOCK_TOKENS]


def attend(column, slot, queries, keys, values, fetched):
    rows, width = queries.shape
    blocks = rows // BLOCK_TOKENS
    table, first = [], 0
    for f in fetched:
        size = f.shape[1]
        inside = (slot >= first) & (slot < first + size)
        table.append(jnp.where(inside, column * size + slot - first, -1))
        first += size
    order = sorted(range(len(fetched)), key=lambda n: fetched[n].shape[1])
    table = [table[n] for n in order]
    fetched = [fetched[n].reshape(-1, *fetched[n].shape[2:]) for n in order]
    anywhere = pl.BlockSpec(memory_space=pl.ANY)
    on_chip = pl.BlockSpec(memory_space=pltpu.VMEM)
    return pl.pallas_call(
        lambda *refs: attend_kernel(len(fetched), *refs),
        out_shape=jax.ShapeDtypeStruct((rows, width), jnp.bfloat16),
        grid_spec=pltpu.PrefetchScalarGridSpec(
            num_scalar_prefetch=1,
            grid=(blocks,),
            in_specs=[pl.BlockSpec((BLOCK_TOKENS, width), lambda i, s: (i, 0))]
            + [anywhere] * 2
            + [on_chip] * (len(fetched) - 1)
            + [anywhere],
            out_specs=pl.BlockSpec((BLOCK_TOKENS, width), lambda i, s: (i, 0)),
            scratch_shapes=[
                pltpu.VMEM((width // HEAD_SIZE * BLOCK_TOKENS, HEAD_SIZE), jnp.bfloat16),
                pltpu.VMEM((2, PICKED_BLOCKS, 2 * BLOCK_TOKENS, HEAD_SIZE), jnp.bfloat16),
                pltpu.SemaphoreType.DMA((2, PICKED_BLOCKS)),
            ],
        ),
        compiler_params=pltpu.CompilerParams(vmem_limit_bytes=ATTEND_GRANT),
        name="attend",
    )(jnp.stack([t.reshape(-1) for t in table]), queries, keys, values, *fetched)


def flat(x, z, c):
    return (x % SIZE_X * SIZE_Z + z % SIZE_Z) * CORES + c


CHIPS = [(x, z, c) for x in range(SIZE_X) for z in range(SIZE_Z) for c in range(CORES)]
FIRST = [(flat(x, z, c), flat(x, z + 1 - 2 * ((z + c) % 2), c)) for x, z, c in CHIPS]
SECOND = [(flat(x, z, c), flat(x, z - 1 + 2 * ((z + c) % 2), c)) for x, z, c in CHIPS]
ROWS = [[flat(x, z, c) for x in range(SIZE_X) for c in range(CORES)] for z in range(SIZE_Z)]


def to_row(array):
    return lax.all_to_all(array, "ctx", split_axis=0, concat_axis=0, axis_index_groups=ROWS)


def attention(queries, key_vector_rows, value_vector_rows, block_picks):
    blocks = key_vector_rows.shape[0] // BLOCK_TOKENS
    group = SIZE_X * CORES
    my_z = lax.axis_index("ctx") // CORES % SIZE_Z
    owners, local_ids = block_picks // blocks, block_picks % blocks
    owner_x, owner_z, owner_core = owners // (SIZE_Z * CORES), owners // CORES % SIZE_Z, owners % CORES
    distance = owner_z - my_z
    distance = jnp.where((my_z + owner_core) % 2 == 0, distance, -distance) % SIZE_Z
    slot = jnp.zeros_like(distance)
    for s, d in enumerate(OFFSETS):
        slot = jnp.where(distance == d % SIZE_Z, s, slot)
    column = owner_x * CORES + owner_core
    places = column * SIZE_Z + slot
    far = places[:, 1:].reshape(-1)
    far_ids = local_ids[:, 1:].reshape(-1)
    index = jnp.arange(group, dtype=jnp.int32)[:, None] * SIZE_Z + jnp.arange(SIZE_Z, dtype=jnp.int32)[None, :]
    requests = jnp.max(jnp.where(far == index[:, :, None], far_ids, 0), axis=2)
    wanted = to_row(requests)

    shard = pack(key_vector_rows, value_vector_rows)
    other = lax.ppermute(shard, "ctx", FIRST)
    pairs = [jnp.concatenate([shard, other], axis=0)]
    for n in range(1, 4):
        pairs.append(lax.ppermute(pairs[-1], "ctx", SECOND if n % 2 else FIRST))

    origin = {s: (pairs[s // 2], s % 2 * blocks) for s in range(SIZE_Z)}
    fetched = []
    for slots in BATCHES:
        arrays, sources = [], []
        for s in slots:
            array, first = origin[s]
            which = next((i for i, a in enumerate(arrays) if a is array), None)
            if which is None:
                which = len(arrays)
                arrays.append(array)
            sources.append((which, first))
        outgoing = pick_blocks(wanted, slots, sources, arrays)
        fetched.append(to_row(outgoing))
    attended = attend(column, slot, queries, key_vector_rows, value_vector_rows, fetched)
    return lax.all_to_all(attended, "kvh", split_axis=0, concat_axis=1, tiled=True)


def solution(mesh):
    return jax.shard_map(
        attention,
        mesh=mesh,
        in_specs=(P("ctx", "kvh"), P("ctx", "kvh"), P("ctx", "kvh"), P("ctx", None)),
        out_specs=P(("ctx", "kvh"), None),
        check_vma=False,
    )
```
